32 devices in a mesh: dp: 8 (over y, x, core), tensor: 4 (over z).
Axes of the slice: x: 2, y: 2, z: 4, core: 2. Of those that a mesh axis runs over, the one named last changes fastest.
Arguments:
- tokens: bfloat16 [12288, 768], P('dp'), may hold values from -6 to 6
- lengths: int32 [8, 3], P('dp'), may hold values from 1 to 1024, 1536 in all within a row
- deal_order: int32 [12288], P('dp'), may hold values from 0 to 12287, as said below
- w_qkv: float32 [3, 768, 768], P(None, None, 'tensor'), may hold values from -0.21875 to 0.21875
- b_qv: float32 [2, 768], P(None, 'tensor'), may hold values from -3 to 3
- w_out: float32 [768, 768], P('tensor'), may hold values from -2.5 to 2.5
- b_out: float32 [768], replicated, may hold values from -2 to 2
- ln1_gain: float32 [768], replicated, may hold values from 0.5 to 1.5
- ln1_bias: float32 [768], replicated, may hold values from -2 to 2
- w_up: float32 [768, 3072], P(None, 'tensor'), may hold values from -0.21875 to 0.21875
- b_up: float32 [3072], P('tensor'), may hold values from -3 to 3
- w_down: float32 [3072, 768], P('tensor'), may hold values from -0.109375 to 0.109375
- b_down: float32 [768], replicated, may hold values from -2 to 2
- ln2_gain: float32 [768], replicated, may hold values from 0.5 to 1.5
- ln2_bias: float32 [768], replicated, may hold values from -2 to 2
- cotangent: bfloat16 [12288, 768], P('dp'), may hold values from -6 to 6
Outputs:
- output: bfloat16 [12288, 768], P('dp')
- input_grad: bfloat16 [12288, 768], P('dp')
- grad_w_qkv: float32 [3, 768, 768], P(None, None, 'tensor')
- grad_b_qv: float32 [2, 768], P(None, 'tensor')
- grad_w_out: float32 [768, 768], P('tensor')
- grad_b_out: float32 [768], replicated
- grad_ln1_gain: float32 [768], replicated
- grad_ln1_bias: float32 [768], replicated
- grad_w_up: float32 [768, 3072], P(None, 'tensor')
- grad_b_up: float32 [3072], P('tensor')
- grad_w_down: float32 [3072, 768], P('tensor')
- grad_b_down: float32 [768], replicated
- grad_ln2_gain: float32 [768], replicated
- grad_ln2_bias: float32 [768], replicated
The draws below stay inside these ranges and needn't reach their ends.
Inputs may be any that keep to these rules, and one draw needn't show every extreme that they name: deal_order is a permutation of 0 to 12287. With b = 192, the token in row t of the s-th block of 1536 rows goes to a position p with (p mod 1536) // b equal to s. Each row of lengths sums to 1536.
All inputs are finite; a program needn't handle non-finite values.
Results may differ from the reference program's by a relative error of at most 0.02.
Values may be sent and summed in bfloat16 or wider, within the bound.
A program may use at most 128 MiB of HBM per device.

```python
import math
import jax
import jax.numpy as jnp
import numpy as np
from jax import lax

D = 768
H = 12
HD = 64
FF = 3072
SEQ_DEV = 3
LONGEST = 1024
TOK_DEV = 1536
TOKENS = 12288
N_DP = 8


def draw_deal_order(key, part):
    groups = TOKENS // TOK_DEV
    block_len = TOK_DEV // groups
    key_list = jax.random.split(jax.random.fold_in(key, 17), groups)
    shuffled = jax.vmap(lambda one_key: jax.random.permutation(one_key, TOK_DEV))(key_list).astype(jnp.int32)
    sources = jnp.arange(groups, dtype=jnp.int32)[:, None]
    dealt_pos = shuffled // block_len * TOK_DEV + sources * block_len + shuffled % block_len
    return dealt_pos.reshape(-1).astype(jnp.int32)


def levels(rng, shape, cuts, smallest, top_value):
    def one(dim, blocks):
        heights = jax.random.uniform(jax.random.fold_in(jax.random.fold_in(rng, 6), dim), (blocks,), jnp.float32, smallest / len(cuts), top_value / len(cuts))
        return jnp.repeat(jnp.exp(heights), shape[dim] // blocks).reshape((-1,) + (1,) * (len(shape) - dim - 1))

    loudness = one(*cuts[0])
    for cut in cuts[1:]:
        loudness = loudness * one(*cut)
    return loudness


def profile(count, total, limit, lean):
    portions = [(1 << 20) // math.isqrt(rank ** lean) + 1 for rank in range(2, count + 1)]
    rest, counts = total - limit - (count - 1), [1] * (count - 1)
    while rest > 0:
        free = [i for i in range(count - 1) if counts[i] < limit]
        mass, budget = sum([portions[i] for i in free]), rest
        for i in free:
            extra = min(limit - counts[i], max(1, budget * portions[i] // mass), rest)
            counts[i] = counts[i] + extra
            rest = rest - extra
    return np.array([limit] + counts)


def ragged_sizes(rng, number_of, total, reach, slope):
    if number_of == 2:
        one = jax.random.randint(rng, (), max(1, total - reach), min(reach, total - 1) + 1)
        return jnp.stack([one, total - one])
    sizes = jnp.asarray(profile(number_of, total, reach, slope), jnp.int32)
    pairs = (number_of - 1) // 2
    source_of, taker = sizes[1:1 + 2 * pairs:2], sizes[2:2 + 2 * pairs:2]
    margin = jnp.minimum(source_of - 1, reach - taker)
    shifted = jax.random.randint(jax.random.fold_in(rng, 1), (pairs,), 0, 1 << 20) % (margin + 1)
    sizes = sizes.at[1:1 + 2 * pairs:2].set(source_of - shifted).at[2:2 + 2 * pairs:2].set(taker + shifted)
    return sizes[jax.random.permutation(jax.random.fold_in(rng, 2), number_of)]


def noise(key, shape, width, most, cuts=(), held_as=jnp.bfloat16):
    level = levels(key, shape, cuts, -0.22, 0.18) if cuts else 1.0
    values = jax.random.normal(key, shape, jnp.float32) * width * level
    return jnp.minimum(jnp.maximum(values, -most), most).astype(held_as)


def setup_inputs(seed: int = 0) -> dict:
    arg_keys = jax.random.split(jax.random.key(seed), 17)
    tokens = noise(arg_keys[0], (TOKENS, D), 1.0, 6.0, ((0, 8),))
    lengths = jax.vmap(lambda own: ragged_sizes(own, SEQ_DEV, TOK_DEV, LONGEST, 2))(jax.random.split(arg_keys[1], N_DP)).reshape((N_DP, SEQ_DEV)).astype(jnp.int32)
    deal_order = draw_deal_order(jax.random.fold_in(arg_keys[16], 71), 0)
    w_qkv = noise(arg_keys[3], (3, D, D), D ** -0.5, 0.21875, ((2, 4),), jnp.float32)
    b_qv = noise(arg_keys[4], (2, D), 0.5, 3.0, ((1, 4),), jnp.float32)
    w_out = noise(arg_keys[5], (D, D), (max(D // 128, 1)) ** -0.5, 2.5, ((0, 4),), jnp.float32)
    b_out = noise(arg_keys[6], (D,), 0.3, 2.0, (), jnp.float32)
    ln1_gain = jnp.clip(1.0 + 0.1 * jax.random.normal(arg_keys[7], (D,), jnp.float32), 0.5, 1.5)
    ln1_bias = noise(arg_keys[8], (D,), 0.3, 2.0, (), jnp.float32)
    w_up = noise(arg_keys[9], (D, FF), D ** -0.5, 0.21875, ((1, 4),), jnp.float32)
    b_up = noise(arg_keys[10], (FF,), 0.5, 3.0, ((0, 4),), jnp.float32)
    w_down = noise(arg_keys[11], (FF, D), FF ** -0.5, 0.109375, ((0, 4),), jnp.float32)
    b_down = noise(arg_keys[12], (D,), 0.3, 2.0, (), jnp.float32)
    ln2_gain = jnp.clip(1.0 + 0.1 * jax.random.normal(arg_keys[13], (D,), jnp.float32), 0.5, 1.5)
    ln2_bias = noise(arg_keys[14], (D,), 0.3, 2.0, (), jnp.float32)
    cotangent = noise(arg_keys[15], (TOKENS, D), 1.0, 6.0, ((0, 8),))
    return {"tokens": tokens, "lengths": lengths, "deal_order": deal_order, "w_qkv": w_qkv, "b_qv": b_qv, "w_out": w_out, "b_out": b_out, "ln1_gain": ln1_gain, "ln1_bias": ln1_bias, "w_up": w_up, "b_up": b_up, "w_down": w_down, "b_down": b_down, "ln2_gain": ln2_gain, "ln2_bias": ln2_bias, "cotangent": cotangent}


@jax.custom_vjp
def low(v):
    return lax.optimization_barrier(v.astype(jnp.bfloat16)).astype(jnp.float32)

@jax.custom_vjp
def low_back(v):
    return v

def low_keep(v):
    return (low(v), None)

def low_pass(kept, grad):
    return (grad,)

def back_keep(v):
    return (v, None)

def back_low(kept, grad):
    return (low(grad),)
low.defvjp(low_keep, low_pass)
low_back.defvjp(back_keep, back_low)
precise = lax.Precision.HIGHEST

def matmul(left, right):
    return jnp.dot(left, right, precision=precise)

def layer_norm(summed, gain_vec, bias_vec):
    average = lax.optimization_barrier(jnp.mean(summed, axis=-1, keepdims=True))
    centered = summed - average
    variance = lax.optimization_barrier(jnp.mean(centered * centered, axis=-1, keepdims=True))
    return centered * lax.rsqrt(variance + 1e-06) * gain_vec + bias_vec

def encoder_group(params, group):
    inputs, row_lengths = group
    w_qkv, b_qv, w_out, b_out, ln1_gain, ln1_bias, w_up, b_up, w_down, b_down, ln2_gain, ln2_bias = params
    positions = jnp.arange(TOK_DEV, dtype=jnp.int32)
    seq_ends = jnp.cumsum(row_lengths, dtype=jnp.int32)
    segment_id = lax.optimization_barrier(jnp.sum((positions[:, None] >= seq_ends[None, :]).astype(jnp.int32), axis=1))
    same_doc = segment_id[:, None] == segment_id[None, :]
    projected = jnp.einsum('td,cde->cte', inputs, low(w_qkv), precision=precise)
    biases = low(b_qv)
    query_low = low(low_back((projected[0] + biases[0]) * HD ** (-0.5))).reshape(TOK_DEV, H, HD)
    key_low = low(low_back(projected[1])).reshape(TOK_DEV, H, HD)
    value_low = low(low_back(projected[2] + biases[1])).reshape(TOK_DEV, H, HD)
    scores = low_back(jnp.einsum('qhd,khd->hqk', query_low, key_low, precision=precise))
    scores = jnp.where(same_doc[None], scores, -1000000000.0)
    row_max = lax.optimization_barrier(jnp.max(scores, axis=-1, keepdims=True))
    exp_scores = jnp.exp(scores - row_max)
    probs_low = low(exp_scores / lax.optimization_barrier(jnp.sum(exp_scores, axis=-1, keepdims=True)))
    mixed = jnp.einsum('hqk,khd->qhd', probs_low, value_low, precision=precise).reshape(TOK_DEV, D)
    attended = low(low_back(mixed))
    sum_first = low_back(matmul(attended, low(w_out))) + low(b_out) + inputs
    hidden = layer_norm(sum_first, ln1_gain, ln1_bias)
    up_input = low_back(matmul(low(hidden), low(w_up)) + low(b_up))
    activated = jax.nn.gelu(up_input, approximate=False)
    sum_second = low_back(matmul(low(activated), low(w_down))) + low(b_down) + hidden
    return layer_norm(sum_second, ln2_gain, ln2_bias)

def reference(tokens, lengths, deal_order, w_qkv, b_qv, w_out, b_out, ln1_gain, ln1_bias, w_up, b_up, w_down, b_down, ln2_gain, ln2_bias, cotangent):
    dealt = jnp.zeros_like(tokens).at[deal_order].set(tokens).astype(jnp.float32).reshape(N_DP, TOK_DEV, D)
    dealt_cot = jnp.zeros_like(cotangent).at[deal_order].set(cotangent).astype(jnp.float32).reshape(N_DP, TOK_DEV, D)
    params = jax.tree.map(lambda array: array.astype(jnp.float32), (w_qkv, b_qv, w_out, b_out, ln1_gain, ln1_bias, w_up, b_up, w_down, b_down, ln2_gain, ln2_bias))

    def forward(params_in, inputs_in):
        return lax.map(jax.checkpoint(lambda group: encoder_group(params_in, group)), (inputs_in, lengths))
    results, pullback = jax.vjp(forward, params, dealt)
    grad_params, grad_inputs = pullback(dealt_cot)
    output = results.reshape(TOKENS, D)[deal_order].astype(jnp.bfloat16)
    input_grad = grad_inputs.reshape(TOKENS, D)[deal_order].astype(jnp.bfloat16)
    return (output, input_grad, grad_params[0], grad_params[1], grad_params[2], grad_params[3], grad_params[4], grad_params[5], grad_params[6], grad_params[7], grad_params[8], grad_params[9], grad_params[10], grad_params[11])
```

```python
import functools
import math

import jax
import jax.numpy as jnp
from jax import lax
from jax.experimental import pallas as pl
from jax.experimental.pallas import tpu as pltpu
from jax.sharding import PartitionSpec as P

HD = 64
QUAD = 4
OCT = 8
BF = jnp.bfloat16
F32 = jnp.float32
MESH = pl.DeviceIdType.MESH
ANY = pl.BlockSpec(memory_space=pl.ANY)
VM = pl.BlockSpec(memory_space=pltpu.VMEM)
NEG = -1000000000.0


def params(limit=56, **kw):
    return pltpu.CompilerParams(vmem_limit_bytes=limit * 2**20, **kw)


def xs(a, k):
    if k & 1:
        a = a + 1 - 2 * (a % 2)
    if k & 2:
        a = a + 2 - 4 * ((a // 2) % 2)
    if k & 4:
        a = a + 4 - 8 * ((a // 4) % 2)
    return a


def xt(a, b):
    return (a + b) % 2 + 2 * ((a // 2 + b // 2) % 2)


def dot(a, b, ca=1, cb=0):
    return lax.dot_general(a, b, (((ca,), (cb,)), ((), ())), preferred_element_type=F32)


def pick_kernel(row_ref, tok_ref, cot_ref, tok_out, cot_out):
    rows = tok_out.shape[0]
    first = pl.program_id(0) * rows
    want = lax.broadcasted_iota(jnp.int32, (rows, 1), 0) + first
    hot = (want == row_ref[...]).astype(F32).astype(BF)
    tok_out[...] = dot(hot, tok_ref[...]).astype(BF)
    cot_out[...] = dot(hot, cot_ref[...]).astype(BF)


def pick_rows(row, tokens, cot, rows):
    n, width = tokens.shape
    blk = 128
    return pl.pallas_call(
        pick_kernel,
        grid=(rows // blk,),
        in_specs=[
            pl.BlockSpec((1, n), lambda i: (0, 0)),
            pl.BlockSpec((n, width), lambda i: (0, 0)),
            pl.BlockSpec((n, width), lambda i: (0, 0)),
        ],
        out_specs=[pl.BlockSpec((blk, width), lambda i: (i, 0))] * 2,
        out_shape=[jax.ShapeDtypeStruct((rows, width), BF)] * 2,
        compiler_params=params(),
        name="pick",
    )(row.reshape(1, n), tokens, cot)


def place_kernel(row_ref, rows_ref, out_ref):
    n = rows_ref.shape[0]
    blk = out_ref.shape[0]
    have = lax.broadcasted_iota(jnp.int32, (blk, n), 1)
    hot = (have == row_ref[...]).astype(F32).astype(BF)
    out_ref[...] = dot(hot, rows_ref[...]).astype(BF)


def place_rows(row, rows):
    n, width = rows.shape
    blk = 256
    return pl.pallas_call(
        place_kernel,
        grid=(n // blk,),
        in_specs=[
            pl.BlockSpec((blk, 1), lambda i: (i, 0)),
            pl.BlockSpec((n, width), lambda i: (0, 0)),
        ],
        out_specs=pl.BlockSpec((blk, width), lambda i: (i, 0)),
        out_shape=jax.ShapeDtypeStruct((n, width), BF),
        compiler_params=params(),
        name="place",
    )(row.reshape(n, 1), rows)


def deal_kernel(
    G, tok_ref, cot_ref, len_ref, wq_ref, bq_ref,
    xg_ref, cown_ref, len_out, wq_out, bq_out,
    s_a, r_a, s_b, r_b, s_c, r_c, s_d, r_d, s_e, r_e, s_f, r_f, loc,
):
    dp = lax.axis_index("dp")
    t = lax.axis_index("tensor")
    nq = G // QUAD
    m, par, quad, o = dp % 4, dp % 2, dp // 4, dp % 8
    base = dp - o

    def remote(src, dst, ss, rs, to_dp, to_t):
        return pltpu.make_async_remote_copy(
            src_ref=src, dst_ref=dst, send_sem=ss, recv_sem=rs,
            device_id=(to_dp, to_t), device_id_type=MESH,
        )

    def start(copy, local, is_self):
        @pl.when(is_self)
        def _():
            local.start()

        @pl.when(jnp.logical_not(is_self))
        def _():
            copy.start()

    sends_a = []
    for tp in range(4):
        for h in range(2):
            to = base + 4 * h + xs(t, tp)
            own = jnp.logical_and(to == dp, t == tp)
            copy = remote(wq_ref, wq_out.at[:, o], s_a.at[2 * tp + h], r_a.at[o], to, tp)
            local = pltpu.make_async_copy(wq_ref, wq_out.at[:, o], loc.at[0])
            start(copy, local, own)
            sends_a.append((copy, local, own))
    line = xt(m, t)
    copy_f = remote(bq_ref, bq_out, s_f, r_f, dp, line)
    local_f = pltpu.make_async_copy(bq_ref, bq_out, loc.at[1])
    own_f = m == 0
    start(copy_f, local_f, own_f)
    sends_e = []
    for j in range(4):
        copy = remote(len_ref, len_out, s_e.at[j], r_e, 4 * quad + j, t)
        local = pltpu.make_async_copy(len_ref, len_out, loc.at[2])
        own = m == j

        @pl.when(m == t)
        def _(copy=copy, local=local, own=own):
            start(copy, local, own)

        sends_e.append((copy, local, own))
    sends_b = []
    for q in range(nq):
        for k in range(2):
            to = 4 * q + par + 2 * k
            own = to == dp
            dst = xg_ref.at[dp // 2, par]
            copy = remote(tok_ref.at[q], dst, s_b.at[2 * q + k], r_b.at[dp // 2], to, t)
            local = pltpu.make_async_copy(tok_ref.at[q], dst, loc.at[3])
            start(copy, local, own)
            sends_b.append((copy, local, own))
    sends_d = []
    for q in range(nq):
        to = 4 * q + dp // nq
        own = to == dp
        dst = cown_ref.at[dp % nq]
        copy = remote(cot_ref.at[q], dst, s_d.at[q], r_d.at[dp % nq], to, t)
        local = pltpu.make_async_copy(cot_ref.at[q], dst, loc.at[4])
        start(copy, local, own)
        sends_d.append((copy, local, own))

    for s in range(G // 2):
        src = 2 * s + par
        dst = xg_ref.at[s, par]

        @pl.when(src != dp)
        def _(dst=dst, s=s, src=src):
            remote(tok_ref.at[0], dst, s_b.at[0], r_b.at[s], src, t).wait_recv()

        @pl.when(src == dp)
        def _(dst=dst):
            pltpu.make_async_copy(tok_ref.at[0], dst, loc.at[3]).wait()

    copy_c = remote(xg_ref.at[:, par], xg_ref.at[:, par], s_c, r_c, xs(dp, 1), t)
    copy_c.start()

    for copy, local, own in sends_a + [(copy_f, local_f, own_f)] + sends_b + sends_d:
        @pl.when(jnp.logical_not(own))
        def _(copy=copy):
            copy.wait_send()

    for copy, local, own in sends_e:
        @pl.when(jnp.logical_and(m == t, jnp.logical_not(own)))
        def _(copy=copy):
            copy.wait_send()

    for i in range(OCT):
        own = jnp.logical_and(o == i, m == 0)
        dst = wq_out.at[:, i]

        @pl.when(own)
        def _(dst=dst):
            pltpu.make_async_copy(wq_ref, dst, loc.at[0]).wait()

        @pl.when(jnp.logical_not(own))
        def _(dst=dst, i=i):
            remote(wq_ref, dst, s_a.at[0], r_a.at[i], base + i, line).wait_recv()

    @pl.when(own_f)
    def _():
        local_f.wait()

    @pl.when(jnp.logical_not(own_f))
    def _():
        copy_f.wait_recv()

    @pl.when(m == t)
    def _():
        pltpu.make_async_copy(len_ref, len_out, loc.at[2]).wait()

    @pl.when(m != t)
    def _():
        remote(len_ref, len_out, s_e.at[0], r_e, 4 * quad + t, t).wait_recv()

    for i in range(nq):
        src = m * nq + i
        dst = cown_ref.at[i]

        @pl.when(src != dp)
        def _(dst=dst, i=i, src=src):
            remote(cot_ref.at[0], dst, s_d.at[0], r_d.at[i], src, t).wait_recv()

        @pl.when(src == dp)
        def _(dst=dst):
            pltpu.make_async_copy(cot_ref.at[0], dst, loc.at[4]).wait()

    copy_c.wait()


def deal(G, tok, cot, lens, wq, bq):
    nq = G // QUAD
    b, width = tok.shape[1:]
    dma = pltpu.SemaphoreType.DMA
    return pl.pallas_call(
        functools.partial(deal_kernel, G),
        in_specs=[ANY] * 5,
        out_specs=[ANY] * 5,
        out_shape=[
            jax.ShapeDtypeStruct((G // 2, 2, b, width), BF),
            jax.ShapeDtypeStruct((nq, b, width), BF),
            jax.ShapeDtypeStruct(lens.shape, lens.dtype),
            jax.ShapeDtypeStruct((wq.shape[0], OCT) + wq.shape[1:], BF),
            jax.ShapeDtypeStruct(bq.shape, bq.dtype),
        ],
        scratch_shapes=[
            dma((8,)), dma((8,)), dma((2 * nq,)), dma((G // 2,)), dma, dma,
            dma((nq,)), dma((nq,)), dma((4,)), dma, dma, dma, dma((5,)),
        ],
        compiler_params=params(has_side_effects=True),
        name="deal",
    )(tok, cot, lens, wq, bq)


def doc_range(ends, row):
    first, last = 0, ends[-1]
    for e in ends[:-1]:
        first = jnp.where(row >= e, e, first)
    for e in reversed(ends[:-1]):
        last = jnp.where(row < e, e, last)
    return first, last


def segments(ends, rows):
    seg = jnp.zeros(rows.shape, jnp.int32)
    for e in ends[:-1]:
        seg = seg + (rows >= e).astype(jnp.int32)
    return seg


def read_ends(sc_ref, docs, total):
    ends, run = [], 0
    for d in range(docs - 1):
        run = run + sc_ref[d]
        ends.append(run)
    return ends + [total]


def half_mask(rows, upper):
    lane = lax.broadcasted_iota(jnp.int32, (rows, 2 * HD), 1)
    return (lane >= HD) if upper else (lane < HD)


def attn_fwd_kernel(docs, bq_rows, bk_rows, sc_ref, x_ref, w_ref, bias_ref, o0, o1, o2, o3, lse_ref, q_ref, k_ref, v_ref, o_s):
    n = x_ref.shape[0]
    own = o0.shape[0]
    m = lax.axis_index("dp") % 4
    scale = HD ** (-0.5)
    ends = read_ends(sc_ref, docs, n)

    def project(i, _):
        rows = pl.ds(pl.multiple_of(i * 256, 256), 256)
        xb = x_ref[rows, :]
        q_ref[rows, :] = ((dot(xb, w_ref[0]) + bias_ref[0:1, :]) * scale).astype(BF)
        k_ref[rows, :] = dot(xb, w_ref[1]).astype(BF)
        v_ref[rows, :] = (dot(xb, w_ref[2]) + bias_ref[1:2, :]).astype(BF)
        return 0

    lax.fori_loop(0, n // 256, project, 0)

    def q_block(i, _):
        r0 = pl.multiple_of(i * bq_rows, bq_rows)
        rows = pl.ds(r0, bq_rows)
        lo, _u = doc_range(ends, r0)
        _u, hi = doc_range(ends, r0 + bq_rows - 1)
        seg_q = segments(ends, r0 + lax.broadcasted_iota(jnp.int32, (bq_rows, 1), 0))
        qt = q_ref[rows, 0 : 2 * HD]
        zero = jnp.zeros_like(qt)
        qh = [
            jnp.where(half_mask(bq_rows, False), qt, zero),
            jnp.where(half_mask(bq_rows, True), qt, zero),
            q_ref[rows, 2 * HD : 3 * HD],
        ]

        def k_block(j, carry):
            k0 = pl.multiple_of(j * bk_rows, bk_rows)
            keys = pl.ds(k0, bk_rows)
            seg_k = segments(ends, k0 + lax.broadcasted_iota(jnp.int32, (1, bk_rows), 1))
            same = seg_q == seg_k
            out = []
            for h in range(3):
                cols = slice(0, 2 * HD) if h < 2 else slice(2 * HD, 3 * HD)
                mx, total, acc = carry[h]
                s = jnp.where(same, dot(qh[h], k_ref[keys, cols], 1, 1), NEG)
                new = jnp.maximum(mx, jnp.max(s, axis=1, keepdims=True))
                p = jnp.exp(s - new)
                alpha = jnp.exp(mx - new)
                total = alpha * total + jnp.sum(p, axis=1, keepdims=True)
                acc = alpha * acc + dot(p.astype(BF), v_ref[keys, cols])
                out.append((new, total, acc))
            return tuple(out)

        init = tuple(
            (
                jnp.full((bq_rows, 1), NEG, F32),
                jnp.zeros((bq_rows, 1), F32),
                jnp.zeros((bq_rows, 2 * HD if h < 2 else HD), F32),
            )
            for h in range(3)
        )
        res = lax.fori_loop(lo // bk_rows, (hi + bk_rows - 1) // bk_rows, k_block, init)
        heads = [acc / total for _m, total, acc in res]
        o_s[rows, 0 : 2 * HD] = jnp.where(half_mask(bq_rows, True), heads[1], heads[0]).astype(BF)
        o_s[rows, 2 * HD : 3 * HD] = heads[2].astype(BF)
        lane = lax.broadcasted_iota(jnp.int32, (bq_rows, 128), 1)
        stat = jnp.zeros((bq_rows, 128), F32)
        for h in range(3):
            mx, total, _a = res[h]
            stat = jnp.where(lane == h, mx + jnp.log(total), stat)
        lse_ref[rows, :] = stat
        return 0

    lax.fori_loop(0, n // bq_rows, q_block, 0)
    for j, ref in enumerate((o0, o1, o2, o3)):
        ref[...] = o_s[pl.ds(pl.multiple_of(xs(m, j) * own, own), own), :]


def attn_fwd(lens, x, w, bias):
    n = x.shape[0]
    wid = w.shape[2]
    own = n // QUAD
    sd = jax.ShapeDtypeStruct
    return pl.pallas_call(
        functools.partial(attn_fwd_kernel, lens.shape[0], 256, 256),
        in_specs=[pl.BlockSpec(memory_space=pltpu.SMEM), VM, VM, VM],
        out_specs=[VM] * 8,
        out_shape=[sd((own, wid), BF)] * 4 + [sd((n, 128), F32)] + [sd((n, wid), BF)] * 3,
        scratch_shapes=[pltpu.VMEM((n, wid), BF)],
        compiler_params=params(),
        name="attn_fwd",
    )(lens, x, w, bias)


def attn_bwd_kernel(
    docs, bq_rows, bk_rows, sc_ref, q_ref, k_ref, v_ref, lse_ref, o0, o1, o2, o3, d0, d1, d2, d3, w_ref,
    gq_ref, gk_ref, gv_ref, p0, p1, p2, p3, qm, km, dm, stat_s, dq_s,
):
    n = q_ref.shape[0]
    own = o0.shape[0]
    m = lax.axis_index("dp") % 4
    scale = HD ** (-0.5)
    ends = read_ends(sc_ref, docs, n)
    wide = 2 * HD

    for j, (oj, dj) in enumerate(((o0, d0), (o1, d1), (o2, d2), (o3, d3))):
        blk = own // 128

        def prep(i, _, oj=oj, dj=dj, j=j):
            src = pl.ds(pl.multiple_of(i * 128, 128), 128)
            dst = pl.ds(pl.multiple_of(xs(m, j) * own + i * 128, 128), 128)
            prod = oj[src, :].astype(F32) * dj[src, :].astype(F32)
            lane = lax.broadcasted_iota(jnp.int32, (128, 128), 1)
            stat = lse_ref[dst, :]
            low = half_mask(128, False)
            pt = prod[:, 0:wide]
            sums = [
                jnp.sum(jnp.where(low, pt, 0.0), axis=1, keepdims=True),
                jnp.sum(jnp.where(low, 0.0, pt), axis=1, keepdims=True),
                jnp.sum(prod[:, wide : wide + HD], axis=1, keepdims=True),
            ]
            for h in range(3):
                stat = jnp.where(lane == 3 + h, sums[h], stat)
            stat_s[:, dst] = stat.T[0:8, :]
            for ref, tile in ((qm, q_ref[dst, 0:wide]), (km, k_ref[dst, 0:wide]), (dm, dj[src, 0:wide])):
                zero = jnp.zeros_like(tile)
                ref[0, dst, :] = jnp.where(low, tile, zero)
                ref[1, dst, :] = jnp.where(low, zero, tile)
            pad = jnp.zeros((128, HD), BF)
            qm[2, dst, 0:HD] = q_ref[dst, wide : wide + HD]
            km[2, dst, 0:HD] = k_ref[dst, wide : wide + HD]
            dm[2, dst, 0:HD] = dj[src, wide : wide + HD]
            return 0

        lax.fori_loop(0, blk, prep, 0)

    dq_s[...] = jnp.zeros_like(dq_s)

    def k_block(j, _):
        k0 = pl.multiple_of(j * bk_rows, bk_rows)
        keys = pl.ds(k0, bk_rows)
        lo, _u = doc_range(ends, k0)
        _u, hi = doc_range(ends, k0 + bk_rows - 1)
        seg_k = segments(ends, k0 + lax.broadcasted_iota(jnp.int32, (bk_rows, 1), 0))

        def q_block(i, carry):
            r0 = pl.multiple_of(i * bq_rows, bq_rows)
            rows = pl.ds(r0, bq_rows)
            seg_q = segments(ends, r0 + lax.broadcasted_iota(jnp.int32, (1, bq_rows), 1))
            same = seg_k == seg_q
            st = stat_s[:, rows]
            dk, dv = list(carry[0]), list(carry[1])
            dq = [None, None]
            for h in range(3):
                tile = h // 2
                w = wide if h < 2 else HD
                kh = km[h, keys, 0:w]
                qh = qm[h, rows, 0:w]
                dh = dm[h, rows, 0:w]
                vh = v_ref[keys, 0:wide] if h < 2 else v_ref[keys, wide : wide + HD]
                s = jnp.where(same, dot(kh, qh, 1, 1), NEG)
                p = jnp.exp(s - st[h : h + 1, :])
                g = dot(vh, dh, 1, 1)
                ds = (p * (g - st[3 + h : 4 + h, :])).astype(BF)
                dv[tile] = dv[tile] + dot(p.astype(BF), dh)
                dk[tile] = dk[tile] + dot(ds, qh)
                part = dot(ds, kh, 0, 0)
                dq[tile] = part if dq[tile] is None else dq[tile] + part
            dq_s[rows, 0:wide] += dq[0]
            dq_s[rows, wide : wide + HD] += dq[1]
            return (tuple(dk), tuple(dv))

        zeros = (jnp.zeros((bk_rows, wide), F32), jnp.zeros((bk_rows, HD), F32))
        dk, dv = lax.fori_loop(lo // bq_rows, (hi + bq_rows - 1) // bq_rows, q_block, (zeros, zeros))
        gk_ref[keys, 0:wide] = dk[0].astype(BF)
        gk_ref[keys, wide : wide + HD] = dk[1].astype(BF)
        gv_ref[keys, 0:wide] = dv[0].astype(BF)
        gv_ref[keys, wide : wide + HD] = dv[1].astype(BF)
        return 0

    lax.fori_loop(0, n // bk_rows, k_block, 0)
    gq_ref[...] = (dq_s[...].astype(BF) * scale).astype(BF)

    for j, ref in enumerate((p0, p1, p2, p3)):
        rows = pl.ds(pl.multiple_of(xs(m, j) * own, own), own)
        ref[...] = (
            dot(gq_ref[rows, :], w_ref[0], 1, 1) + dot(gk_ref[rows, :], w_ref[1], 1, 1) + dot(gv_ref[rows, :], w_ref[2], 1, 1)
        ).astype(BF)


def attn_bwd(lens, q, k, v, lse, outs, grads, w):
    n, wid = q.shape
    own = n // QUAD
    width = w.shape[1]
    sd = jax.ShapeDtypeStruct
    return pl.pallas_call(
        functools.partial(attn_bwd_kernel, lens.shape[0], 256, 256),
        in_specs=[pl.BlockSpec(memory_space=pltpu.SMEM)] + [VM] * 13,
        out_specs=[VM] * 7,
        out_shape=[sd((n, wid), BF)] * 3 + [sd((own, width), BF)] * 4,
        scratch_shapes=[
            pltpu.VMEM((3, n, 2 * HD), BF), pltpu.VMEM((3, n, 2 * HD), BF), pltpu.VMEM((3, n, 2 * HD), BF),
            pltpu.VMEM((8, n), F32), pltpu.VMEM((n, wid), F32),
        ],
        compiler_params=params(),
        name="attn_bwd",
    )(lens, q, k, v, lse, *outs, *grads, w)


def quad_kernel(n_pair, *refs):
    src = refs[0:3]
    pair_in = refs[3 : 3 + n_pair]
    dst = refs[3 + n_pair : 6 + n_pair]
    pair_out = refs[6 + n_pair : 6 + 2 * n_pair]
    ss, rs = refs[6 + 2 * n_pair :]
    dp = lax.axis_index("dp")
    t = lax.axis_index("tensor")
    copies = []
    for i in range(3 + n_pair):
        a, b, k = (src[i], dst[i], i + 1) if i < 3 else (pair_in[i - 3], pair_out[i - 3], 1)
        copies.append(
            pltpu.make_async_remote_copy(
                src_ref=a, dst_ref=b, send_sem=ss.at[i], recv_sem=rs.at[i],
                device_id=(xs(dp, k), t), device_id_type=MESH,
            )
        )
    for i in (1, 2, 0):
        copies[i].start()
    for i in range(3, 3 + n_pair):
        copies[i].start()
    for c in copies:
        c.wait()


def quad_exchange(pieces, pair):
    every = list(pieces) + list(pair)
    dma = pltpu.SemaphoreType.DMA
    out = pl.pallas_call(
        functools.partial(quad_kernel, len(pair)),
        in_specs=[ANY] * len(every),
        out_specs=[ANY] * len(every),
        out_shape=[jax.ShapeDtypeStruct(a.shape, a.dtype) for a in every],
        scratch_shapes=[dma((len(every),)), dma((len(every),))],
        compiler_params=params(has_side_effects=True),
        name="quad",
    )(*every)
    return out[:3], out[3:]


def gelu_parts(v):
    z = jnp.abs(v)
    u = 1.0 / (1.0 + (0.3275911 * math.sqrt(0.5)) * z)
    e = jnp.exp(-0.5 * v * v)
    poly = u * (0.5 * 0.254829592 + u * (0.5 * -0.284496736 + u * (0.5 * 1.421413741 + u * (0.5 * -1.453152027 + u * (0.5 * 1.061405429)))))
    tail = poly * e
    phi = jnp.where(v >= 0.0, 1.0 - tail, tail)
    return v * phi, phi + v * e * (1.0 / math.sqrt(2.0 * math.pi))


def ffn_kernel(
    ch, ch_o, nsem,
    a0, a1, a2, a3, x_any, cot_ref, vb_out, vg1, vb1, vb_down, vg2, vb2,
    wu_own, wd_own, wo_own, bu_own,
    z1, c1, y1, e1, z2, c2, y2, e2, sz1, sc1, sy1, se1, sz2, sc2, sy2, se2,
    res_ref, gfirst_ref, gat0, gat1, gat2, gat3, act_ref, gup_ref, hid_ref, gffn_ref, gattn_ref, vec_ref, gbup_ref,
    wu, wd, wo, bu, xo, gp, sem,
):
    dp = lax.axis_index("dp")
    t = lax.axis_index("tensor")
    m, o = dp % 4, dp % 8
    own, width = res_ref.shape
    count = [0]
    copies = {"o": [], "u": [], "d": []}

    def load(kind, src, dst):
        c = pltpu.make_async_copy(src, dst, sem.at[count[0]])
        count[0] += 1
        c.start()
        copies[kind].append(c)

    load("o", x_any.at[pl.ds(pl.multiple_of(m * own, own), own), :], xo)
    load("o", wo_own, wo.at[t])
    for arr, k in ((z1, 0), (sz1, 1), (c1, 2), (sc1, 3)):
        for j in (1, 2, 3):
            dst = wo.at[xs(t, j), pl.ds(pl.multiple_of(xs(m, k) * ch_o, ch_o), ch_o), :]
            load("o", arr.at[j - 1, pl.ds(ch + 16, ch_o), :], dst)
    load("u", wu_own, wu.at[t])
    load("u", bu_own, bu.at[t])
    for j in (1, 2, 3):
        load("u", z1.at[j - 1, pl.ds(ch, 16), :], bu.at[xs(t, j)])
    for kind, w, arrs in (
        ("u", wu, (z1, sz1, c1, sc1, y1, sy1, e1, se1)),
        ("d", wd, (z2, sz2, c2, sc2, y2, sy2, e2, se2)),
    ):
        if kind == "d":
            load("d", wd_own, wd.at[t])
        for k, arr in enumerate(arrs):
            for j in (1, 2, 3):
                dst = w.at[xs(t, j), pl.ds(pl.multiple_of(xs(o, k) * ch, ch), ch), :]
                load(kind, arr.at[j - 1, pl.ds(0, ch), :], dst)

    for c in copies["o"]:
        c.wait()
    attn = jnp.zeros((own, width), F32)
    for j, a in enumerate((a0, a1, a2, a3)):
        attn = attn + dot(a[...], wo[xt(xs(m, j), t)])

    def norm(z):
        mean = jnp.mean(z, axis=1, keepdims=True)
        c = z - mean
        var = jnp.mean(c * c, axis=1, keepdims=True)
        r = lax.rsqrt(var + 1e-06)
        return c * r, r

    n1, r1 = norm(attn + vb_out[...].astype(BF).astype(F32) + xo[...].astype(F32))
    hidden = n1 * vg1[...] + vb1[...]
    hid_ref[...] = hidden.astype(BF)
    for c in copies["u"]:
        c.wait()
    for c in copies["d"]:
        c.wait()

    sub = 256

    def forward(s, acc):
        for p in range(width // sub):
            cols = slice(p * sub, (p + 1) * sub)
            up = dot(hid_ref[...], wu[s, :, cols]) + bu[s, 0:1, cols].astype(F32)
            act, grad = gelu_parts(up)
            act_ref[s, :, cols] = act.astype(BF)
            gp[s, :, cols] = grad
            acc = acc + dot(act.astype(BF), wd[s, cols, :])
        return acc

    ffn = lax.fori_loop(0, 4, forward, jnp.zeros((own, width), F32))
    n2, r2 = norm(ffn + vb_down[...].astype(BF).astype(F32) + hidden)
    res_ref[...] = (n2 * vg2[...] + vb2[...]).astype(BF)
    e = cot_ref[...].astype(F32)

    def norm_back(e, n, r, gain):
        eg = e * gain
        return r * (eg - jnp.mean(eg, axis=1, keepdims=True) - n * jnp.mean(eg * n, axis=1, keepdims=True))

    g_second = norm_back(e, n2, r2, vg2[...])
    vec_ref[...] = jnp.zeros_like(vec_ref)
    vec_ref[4:5, :] = jnp.sum(e * n2, axis=0, keepdims=True)
    vec_ref[5:6, :] = jnp.sum(e, axis=0, keepdims=True)
    vec_ref[3:4, :] = jnp.sum(g_second, axis=0, keepdims=True)
    gffn_ref[...] = g_second.astype(BF)

    def backward(s, acc):
        for p in range(width // sub):
            cols = slice(p * sub, (p + 1) * sub)
            g = (dot(gffn_ref[...], wd[s, cols, :], 1, 1) * gp[s, :, cols]).astype(BF)
            gup_ref[s, :, cols] = g
            gbup_ref[s, 0:1, cols] = jnp.sum(g.astype(F32), axis=0, keepdims=True)
            acc = acc + dot(g, wu[s, :, cols], 1, 1)
        return acc

    g_hidden = lax.fori_loop(0, 4, backward, g_second)
    g_first = norm_back(g_hidden, n1, r1, vg1[...])
    vec_ref[1:2, :] = jnp.sum(g_hidden * n1, axis=0, keepdims=True)
    vec_ref[2:3, :] = jnp.sum(g_hidden, axis=0, keepdims=True)
    vec_ref[0:1, :] = jnp.sum(g_first, axis=0, keepdims=True)
    gfirst_ref[...] = g_first
    gattn_ref[...] = g_first.astype(BF)
    for j, ref in enumerate((gat0, gat1, gat2, gat3)):
        ref[...] = dot(gattn_ref[...], wo[xt(xs(m, j), t)], 1, 1).astype(BF)


def ffn(att, x, cot, vecs, owns, pieces):
    own, wid = att[0].shape
    width = cot.shape[1]
    ch, ch_o = width // OCT, wid // QUAD
    sd = jax.ShapeDtypeStruct
    nsem = 2 + 12 + 2 + 3 + 24 + 1 + 24
    return pl.pallas_call(
        functools.partial(ffn_kernel, ch, ch_o, nsem),
        in_specs=[VM] * 4 + [ANY] + [VM] * 7 + [ANY] * (4 + 16),
        out_specs=[VM] * 13,
        out_shape=[
            sd((own, width), BF), sd((own, width), F32),
            sd((own, wid), BF), sd((own, wid), BF), sd((own, wid), BF), sd((own, wid), BF),
            sd((4, own, width), BF), sd((4, own, width), BF),
            sd((own, width), BF), sd((own, width), BF), sd((own, width), BF),
            sd((8, width), F32), sd((4, 1, width), F32),
        ],
        scratch_shapes=[
            pltpu.VMEM((4, width, width), BF), pltpu.VMEM((4, width, width), BF), pltpu.VMEM((4, wid, width), BF),
            pltpu.VMEM((4, 16, width), BF), pltpu.VMEM((own, width), BF), pltpu.VMEM((4, own, width), F32),
            pltpu.SemaphoreType.DMA((nsem,)),
        ],
        compiler_params=params(60),
        name="ffn",
    )(*att, x, cot, *vecs, *owns, *pieces)


def wgrad_kernel(a0, a1, a2, a3, act_ref, gup_ref, hid_ref, gffn_ref, gattn_ref, du_ref, dd_ref, do_ref):
    m = lax.axis_index("dp") % 4
    t = lax.axis_index("tensor")

    def one(s, _):
        dd_ref[s] = dot(act_ref[s], gffn_ref[...], 0, 0).astype(BF)
        du_ref[s] = dot(hid_ref[...], gup_ref[s], 0, 0).astype(BF)
        return 0

    lax.fori_loop(0, 4, one, 0)
    for j, a in enumerate((a0, a1, a2, a3)):
        do_ref[xt(xs(m, j), t)] = dot(a[...], gattn_ref[...], 0, 0).astype(BF)


def wgrad(att, act, gup, hid, gffn, gattn):
    wid = att[0].shape[1]
    width = hid.shape[1]
    sd = jax.ShapeDtypeStruct
    return pl.pallas_call(
        wgrad_kernel,
        in_specs=[VM] * 9,
        out_specs=[VM] * 3,
        out_shape=[sd((4, width, width), BF), sd((4, width, width), BF), sd((4, wid, width), BF)],
        compiler_params=params(),
        name="wgrad",
    )(*att, act, gup, hid, gffn, gattn)


def on_device(
    tokens, lengths, deal_order, w_qkv, b_qv, w_out, b_out, ln1_gain, ln1_bias,
    w_up, b_up, w_down, b_down, ln2_gain, ln2_bias, cotangent,
):
    G = lax.axis_size("dp")
    T = lax.axis_size("tensor")
    dp = lax.axis_index("dp")
    t = lax.axis_index("tensor")
    n, width = tokens.shape
    b = n // G
    nq = G // QUAD
    own = n // QUAD
    wid = w_qkv.shape[2]
    ch, ch_o = width // OCT, wid // QUAD
    docs = lengths.shape[1]
    m, o, quad = dp % 4, dp % 8, dp // 4

    dpp = lambda x, k: lax.ppermute(x, "dp", [(i, i ^ k) for i in range(G)])
    zpp = lambda x, k: lax.ppermute(x, "tensor", [(i, i ^ k) for i in range(T)])

    group, slot = deal_order // n, deal_order % b
    q_of, t_of = group // T, group % T
    send_row = jnp.where(t_of == t, q_of * b + slot, -1)
    back_row = t_of * own + ((dp % nq - q_of) % nq) * b + slot
    tok_s, cot_s = pick_rows(send_row, tokens, cotangent, own)

    cut = lambda w, start, rows: lax.dynamic_slice_in_dim(w, start, rows, 0).astype(BF)
    bu16 = jnp.broadcast_to(b_up.astype(BF)[None], (16, width))
    first = jnp.concatenate([cut(w_up, o * ch, ch), bu16, cut(w_out, m * ch_o, ch_o)])
    second = cut(w_down, o * ch, ch)
    z1 = jnp.stack([zpp(first, k) for k in (1, 2, 3)])
    z2 = jnp.stack([zpp(second, k) for k in (1, 2, 3)])
    c1, y1 = dpp(z1, 2), dpp(z1[:, :ch], 4)
    e1 = dpp(y1, 2)
    c2, y2 = dpp(z2, 2), dpp(z2, 4)
    e2 = dpp(c2, 4)

    wq_c = lax.dynamic_slice_in_dim(w_qkv, o * ch, ch, 1).astype(BF)
    bq = jnp.zeros((8, wid), F32).at[:2].set(b_qv.astype(BF).astype(F32))
    lens = jnp.zeros((8, 128), jnp.int32).at[0, :docs].set(lengths[0])
    xg, cown, lens_g, wq, bq_g = deal(G, tok_s.reshape(nq, b, width), cot_s.reshape(nq, b, width), lens, wq_c, bq)
    xg = xg.reshape(n, width)
    cown = cown.reshape(own, width)
    wq = wq.reshape(3, width, wid)
    lens3 = lens_g[0, :docs]

    a0, a1, a2, a3, lse, q, k, v = attn_fwd(lens3, xg, wq, bq_g)
    (b1, b2, b3), pair = quad_exchange((a1, a2, a3), (z1, c1, y1, e1, z2, c2, y2, e2))

    row = lambda vec: vec.reshape(1, width)
    vecs = [row(u) for u in (b_out, ln1_gain, ln1_bias, b_down, ln2_gain, ln2_bias)]
    owns = [w_up.astype(BF), w_down.astype(BF), w_out.astype(BF), bu16]
    att = (a0, b1, b2, b3)
    (result, g_first, ga0, ga1, ga2, ga3, act, gup, hid, gffn, gattn, vec, gbup) = ffn(
        att, xg, cown, vecs, owns, [z1, c1, y1, e1, z2, c2, y2, e2] + list(pair)
    )

    def send_back(rows):
        blocks = rows.reshape(nq, b, width)
        got = []
        for s in range(nq):
            pick = lax.dynamic_index_in_dim(blocks, (quad + s) % nq, 0, False)
            perm = [(4 * qq + mm, mm * nq + (qq + s) % nq) for qq in range(nq) for mm in range(4)]
            got.append(lax.ppermute(pick, "dp", perm))
        mine = jnp.concatenate(got)
        return lax.all_gather(mine, "tensor", axis=0, tiled=True)

    h1, h2, h3 = (dpp(g, i) for g, i in ((ga1, 1), (ga2, 2), (ga3, 3)))
    out_rows = send_back(result)
    du, dd, do = wgrad(att, act, gup, hid, gffn, gattn)

    gq, gk, gv, p0, p1, p2, p3 = attn_bwd(lens3, q, k, v, lse, (a0, a1, a2, a3), (ga0, h1, h2, h3), wq)
    s0 = p0.astype(F32) + dpp(p1, 1).astype(F32)
    s2 = (p2.astype(F32) + dpp(p3, 1).astype(F32)).astype(BF)
    g_low = (g_first + s0 + dpp(s2, 2).astype(F32)).astype(BF)
    in_rows = send_back(g_low)

    output = place_rows(back_row, out_rows)
    input_grad = place_rows(back_row, in_rows)

    octs = [[OCT * i + j for j in range(OCT)] for i in range(G // OCT)]
    across = [[OCT * i + j for i in range(G // OCT)] for j in range(OCT)]

    def reduce_weight(part):
        rows = part.shape[1]
        split = part.reshape(4, OCT, rows // OCT, width).swapaxes(0, 1)
        mine = lax.psum_scatter(split, "dp", scatter_dimension=0, axis_index_groups=octs, tiled=True)
        if G > OCT:
            mine = lax.psum(mine, "dp", axis_index_groups=across)
        mine = lax.psum_scatter(mine[0], "tensor", scatter_dimension=0, tiled=True)
        full = lax.all_gather(mine[0], "dp", axis=0, axis_index_groups=octs, tiled=True)
        return full.astype(F32)

    grad_w_up = reduce_weight(du)
    grad_w_down = reduce_weight(dd)
    grad_w_out = reduce_weight(do)
    g3 = jnp.stack([gq, gk, gv])
    dqkv = jnp.einsum("td,cte->cde", xg, g3, preferred_element_type=F32).astype(BF)
    perm = [(d * T + tt, d * T + ((d % 4) ^ tt)) for d in range(G) for tt in range(T)]
    dqkv = lax.ppermute(dqkv, ("dp", "tensor"), perm)
    grad_w_qkv = lax.psum(dqkv, "dp").astype(F32)
    db = jnp.stack([jnp.sum(gq.astype(F32), 0), jnp.sum(gv.astype(F32), 0)])
    db = lax.ppermute(db, ("dp", "tensor"), perm)
    slot_db = jnp.zeros((T, 2, wid), F32)
    slot_db = lax.dynamic_update_index_in_dim(slot_db, db, t, 0)
    small = jnp.concatenate([vec[:6].reshape(-1), gbup.reshape(-1), slot_db.reshape(-1)])
    small = lax.psum(small, ("dp", "tensor"))
    vec = small[: 6 * width].reshape(6, width)
    grad_b_up = lax.dynamic_slice_in_dim(small, 6 * width + t * width, width)
    grad_b_qv = lax.dynamic_slice_in_dim(small, (6 + T) * width + t * 2 * wid, 2 * wid).reshape(2, wid)
    return (
        output, input_grad, grad_w_qkv, grad_b_qv, grad_w_out, vec[0], vec[1], vec[2],
        grad_w_up, grad_b_up, grad_w_down, vec[3], vec[4], vec[5],
    )


def solution(mesh):
    placed = (
        P("dp", None), P("dp", None), P("dp"), P(None, None, "tensor"), P(None, "tensor"), P("tensor", None),
        P(), P(), P(), P(None, "tensor"), P("tensor"), P("tensor", None), P(), P(), P(), P("dp", None),
    )
    return jax.shard_map(
        on_device,
        mesh=mesh,
        in_specs=placed,
        out_specs=(
            P("dp", None), P("dp", None), P(None, None, "tensor"), P(None, "tensor"), P("tensor", None),
            P(), P(), P(), P(None, "tensor"), P("tensor"), P("tensor", None), P(), P(), P(),
        ),
        check_vma=False,
    )
```
